32 devices in a mesh: section: 8 (over z, core), ctx: 4 (over y, x).
Axes of the slice: x: 2, y: 2, z: 4, core: 2. Of those that a mesh axis runs over, the one named last changes fastest.
Arguments:
- gate_q: bfloat16 [8, 512, 4096], P('section', 'ctx'), may hold values from -6 to 6
- gate_k: bfloat16 [8, 512, 4096], P('section', 'ctx'), may hold values from -6 to 6
- value_in: bfloat16 [8, 512, 4096], P('section', 'ctx'), may hold values from -6 to 6
- filter_raw: bfloat16 [8, 512, 4096], P('section', 'ctx'), may hold values from -0.5 to 0.5
- decay_rate: float32 [8, 4096], P('section'), may hold values from 0.25 to 16
- skip_gain: float32 [8, 4096], P('section'), may hold values from -4 to 4
- grad_out: bfloat16 [8, 512, 4096], P('section', 'ctx'), may hold values from -6 to 6
Outputs:
- grad_q: bfloat16 [8, 512, 4096], P('section', 'ctx')
- grad_k: bfloat16 [8, 512, 4096], P('section', 'ctx')
- grad_passed: bfloat16 [8, 512, 4096], P('section', 'ctx')
- filter_grad: bfloat16 [8, 512, 4096], P('section', 'ctx')
- rate_grad: float32 [8, 4096], P('section')
- skip_grad: float32 [8, 4096], P('section')
The draws below stay inside these ranges and needn't reach their ends.
All inputs are finite; a program needn't handle non-finite values.
Results may differ from the reference program's by a relative error of at most 0.013.
Values may be sent and summed in bfloat16 or wider, within the bound.
A program may use at most 128 MiB of HBM per device.

```python
import math
import jax
import jax.numpy as jnp
from jax import lax

CH = 4096
TOK_DEV = 128
NS = 8
BLOCKS = 4
FACTOR = 8
SEQ = 512
FFT = 1024


def shard_levels(own_key, shape, shards, least, high):
    loudness, own = 1.0, jax.random.fold_in(own_key, 6)
    for position, parts in shards:
        heights = jnp.exp(jax.random.uniform(jax.random.fold_in(own, position), (parts,), jnp.float32, least / len(shards), high / len(shards)))
        loudness = loudness * jnp.repeat(heights, shape[position] // parts).reshape([-1 if axis == position else 1 for axis in range(len(shape))])
    return loudness


def noise(key, dims, spread, most, pieces=(), held_as=jnp.bfloat16):
    gain = shard_levels(key, dims, pieces, -0.22, 0.18) if pieces else 1.0
    drawn = jax.random.normal(key, dims, jnp.float32) * spread * gain
    return jnp.minimum(jnp.maximum(drawn, -most), most).astype(held_as)


def setup_inputs(seed: int = 0) -> dict:
    splits = jax.random.split(jax.random.key(seed), 8)
    gate_q = noise(splits[0], (NS, SEQ, CH), 1.0, 6.0, ((0, 8), (1, 4)))
    gate_k = noise(splits[1], (NS, SEQ, CH), 1.0, 6.0, ((0, 8), (1, 4)))
    value_in = noise(splits[2], (NS, SEQ, CH), 1.0, 6.0, ((0, 8), (1, 4)))
    filter_raw = noise(splits[3], (NS, SEQ, CH), (SEQ // 4) ** -0.5, 0.5, ((0, 8), (1, 4)))
    decay_rate = jnp.clip(jnp.exp(math.log(16.0) - 4.158883 * jax.random.uniform(splits[4], (NS, CH), jnp.float32) ** shard_levels(splits[4], (NS, CH), ((0, 8),), -0.2, 0.2)), 0.25, 16.0)
    skip_gain = noise(splits[5], (NS, CH), 1.0, 4.0, ((0, 8),), jnp.float32)
    grad_out = noise(splits[6], (NS, SEQ, CH), 1.0, 6.0, ((0, 8), (1, 4)))
    return dict(gate_q=gate_q, gate_k=gate_k, value_in=value_in, filter_raw=filter_raw, decay_rate=decay_rate, skip_gain=skip_gain, grad_out=grad_out)


def round_trip(values):
    return lax.optimization_barrier(values.astype(jnp.bfloat16)).astype(jnp.float32)


def twist_angle():
    bins = jnp.arange(FACTOR, dtype=jnp.int32)[:, None]
    rows = jnp.arange(TOK_DEV, dtype=jnp.int32)[None, :]
    product = (bins * rows) % FFT
    angle = product.astype(jnp.float32) * (2.0 * math.pi / FFT)
    return jnp.cos(angle)[:, :, None], jnp.sin(angle)[:, :, None]


def forward_spectrum(signal):
    blocks = signal.astype(jnp.float32).reshape(BLOCKS, TOK_DEV, CH)
    padded = jnp.concatenate([blocks, jnp.zeros_like(blocks)], axis=0)
    partial_value = jnp.fft.fft(padded, axis=0)
    part_real = round_trip(jnp.real(partial_value))
    part_imag = round_trip(jnp.imag(partial_value))
    twist_cos, twist_sin = twist_angle()
    turned = lax.complex(part_real * twist_cos + part_imag * twist_sin,
                         part_imag * twist_cos - part_real * twist_sin)
    return jnp.fft.fft(turned, axis=1)


def inverse_spectrum(spectrum):
    back = jnp.fft.ifft(spectrum, axis=1) * TOK_DEV
    back_real = jnp.real(back)
    back_imag = jnp.imag(back)
    twist_cos, twist_sin = twist_angle()
    fold_real = round_trip(back_real * twist_cos - back_imag * twist_sin)
    fold_imag = round_trip(back_real * twist_sin + back_imag * twist_cos)
    summed = jnp.fft.ifft(lax.complex(fold_real, fold_imag), axis=0) * FACTOR
    values = jnp.real(summed)[:BLOCKS] / FFT
    return values.reshape(SEQ, CH).astype(jnp.bfloat16)


def one_section(inputs):
    gate_q, gate_k, value_in, filter_raw, decay_rate, skip_gain, grad_out = inputs
    positions = (jnp.arange(SEQ, dtype=jnp.int32).astype(jnp.float32) / SEQ)[:, None]
    envelope = jnp.exp(-decay_rate[None, :] * positions)
    modulated = filter_raw.astype(jnp.float32) * envelope
    filter_bf = modulated.astype(jnp.bfloat16)
    mixed_in = (gate_k.astype(jnp.float32) * value_in.astype(jnp.float32)).astype(jnp.bfloat16)
    pulled = (gate_q.astype(jnp.float32) * grad_out.astype(jnp.float32)).astype(jnp.bfloat16)
    spec_mixed = forward_spectrum(mixed_in)
    spec_filter = forward_spectrum(filter_bf)
    spec_pulled = forward_spectrum(pulled)
    conv_out = inverse_spectrum(spec_filter * spec_mixed).astype(jnp.float32)
    adjoint = inverse_spectrum(jnp.conj(spec_filter) * spec_pulled).astype(jnp.float32)
    filter_corr = inverse_spectrum(jnp.conj(spec_mixed) * spec_pulled).astype(jnp.float32)
    skip_row = skip_gain[None, :]
    mixed_f = mixed_in.astype(jnp.float32)
    pulled_f = pulled.astype(jnp.float32)
    grad_q = (grad_out.astype(jnp.float32) * (conv_out + skip_row * mixed_f)).astype(jnp.bfloat16)
    mixed_grad = adjoint + skip_row * pulled_f
    grad_k = (mixed_grad * value_in.astype(jnp.float32)).astype(jnp.bfloat16)
    passing = (mixed_grad * gate_k.astype(jnp.float32)).astype(jnp.bfloat16)
    filter_grad = (filter_corr * envelope).astype(jnp.bfloat16)
    rate_grad = -jnp.sum(positions * filter_corr * modulated, axis=0)
    skip_grad = jnp.sum(mixed_f * pulled_f, axis=0)
    return grad_q, grad_k, passing, filter_grad, rate_grad, skip_grad


def reference(gate_q, gate_k, value_in, filter_raw, decay_rate, skip_gain, grad_out):
    grad_q, grad_k, passing, filter_grad, rate_grad, skip_grad = lax.map(
        one_section, (gate_q, gate_k, value_in, filter_raw, decay_rate, skip_gain, grad_out))
    grad_passed = jnp.concatenate([passing[1:], jnp.zeros_like(passing[:1])], axis=0)
    return grad_q, grad_k, grad_passed, filter_grad, rate_grad, skip_grad
```

```python
import functools
import math

import jax
import jax.numpy as jnp
import numpy as np
from jax import lax
from jax.experimental import pallas as pl
from jax.experimental.pallas import tpu as pltpu
from jax.sharding import PartitionSpec as P

MESH = pl.DeviceIdType.MESH
F32 = jnp.float32
BF16 = jnp.bfloat16


def make_tables(n, rows):
    length = 2 * n * rows
    half = rows // 2
    j = np.arange(rows)[None, :]
    b = np.arange(rows)[:, None]

    def angle(a):
        return 2.0 * np.pi * ((j * (a + 2 * n * b)) % length) / length

    fwd = np.zeros((n, 2 * rows, 2 * rows))
    inv = np.zeros((n, 2 * rows, 2 * rows))
    for a in range(1, n):
        c, s = np.cos(angle(a)), np.sin(angle(a))
        fwd[a] = np.block([[c, s], [-s, c]])
        inv[a] = np.block([[c.T, -s.T], [s.T, c.T]]) * (2.0 / length)
    for slot, a in ((0, 0), (1, n)):
        c, s = np.cos(angle(a))[:half], np.sin(angle(a))[:half]
        weight = np.full((half, 1), 2.0 / length)
        re_rows = slice(slot * half, (slot + 1) * half)
        im_rows = slice(rows + slot * half, rows + (slot + 1) * half)
        cols = slice(slot * rows, (slot + 1) * rows)
        im = -s
        if slot == 0:
            im = im.copy()
            im[0] = np.cos(np.pi * np.arange(rows))
            weight[0] = 1.0 / length
        fwd[0, re_rows, cols] = c
        fwd[0, im_rows, cols] = im
        inv[0, cols, re_rows] = (c * weight).T
        inv[0, cols, im_rows] = (im * weight).T
    return fwd, inv


def scaled(coef, x):
    if abs(coef - 1.0) < 1e-12:
        return x
    if abs(coef + 1.0) < 1e-12:
        return -x
    return x * np.float32(coef)


def combine(terms, zero):
    total = None
    for coef, x in terms:
        if abs(coef) < 1e-12:
            continue
        if total is None:
            total = scaled(coef, x)
        elif coef < 0:
            total = total - scaled(-coef, x)
        else:
            total = total + scaled(coef, x)
    return zero if total is None else total


def kernel(
    n, nsec, chunk, steps,
    gq_ref, gk_ref, vi_ref, fr_ref, go_ref, rate_ref, skip_ref, fwd_ref, inv_ref,
    oq_ref, ok_ref, op_ref, of_ref, orate_ref, oskip_ref,
    sbuf, rbuf, obuf, hbuf, pbuf, part, fold, sstat, gstat,
    s_send, s_recv, o_send, o_recv, p_send, p_recv, t_send, t_recv,
):
    rows = gq_ref.shape[0]
    width = chunk * steps
    seq = rows * n
    me = lax.axis_index("ctx")
    sec = lax.axis_index("section")
    before = lax.rem(sec + nsec - 1, nsec)
    after = lax.rem(sec + 1, nsec)

    barrier = pltpu.get_barrier_semaphore()
    for o in range(1, n):
        pl.semaphore_signal(
            barrier, inc=1, device_id={"ctx": lax.rem(me + o, n)}, device_id_type=MESH
        )
    for other in (before, after):
        pl.semaphore_signal(barrier, inc=1, device_id={"section": other}, device_id_type=MESH)
    pl.semaphore_wait(barrier, n + 1)

    def columns(owner, k):
        return pl.ds(pl.multiple_of(owner * width + k * chunk, chunk), chunk)

    def here(row0, count):
        row = lax.broadcasted_iota(jnp.int32, (count, 1), 0) + (row0 + me * rows)
        return row.astype(F32) * np.float32(1.0 / seq)

    def send_in(k, d):
        return pltpu.make_async_remote_copy(
            src_ref=sbuf.at[k, d], dst_ref=rbuf.at[k, me], send_sem=s_send.at[k, d],
            recv_sem=s_recv.at[k, me], device_id={"ctx": d}, device_id_type=MESH,
        )

    def got_in(k, m):
        return pltpu.make_async_remote_copy(
            src_ref=sbuf.at[k, m], dst_ref=rbuf.at[k, m], send_sem=s_send.at[k, m],
            recv_sem=s_recv.at[k, m], device_id={"ctx": m}, device_id_type=MESH,
        )

    def send_out(k, m):
        return pltpu.make_async_remote_copy(
            src_ref=obuf.at[k, m], dst_ref=hbuf.at[k, me], send_sem=o_send.at[k, m],
            recv_sem=o_recv.at[k, me], device_id={"ctx": m}, device_id_type=MESH,
        )

    def got_out(k, m):
        return pltpu.make_async_remote_copy(
            src_ref=obuf.at[k, m], dst_ref=hbuf.at[k, m], send_sem=o_send.at[k, m],
            recv_sem=o_recv.at[k, m], device_id={"ctx": m}, device_id_type=MESH,
        )

    def send_stat(d):
        return pltpu.make_async_remote_copy(
            src_ref=sstat, dst_ref=gstat.at[me], send_sem=t_send.at[d],
            recv_sem=t_recv.at[me], device_id={"ctx": d}, device_id_type=MESH,
        )

    def got_stat(m):
        return pltpu.make_async_remote_copy(
            src_ref=sstat, dst_ref=gstat.at[m], send_sem=t_send.at[m],
            recv_sem=t_recv.at[m], device_id={"ctx": m}, device_id_type=MESH,
        )

    def pass_copy(k, m):
        return pltpu.make_async_remote_copy(
            src_ref=pbuf.at[k, m], dst_ref=op_ref.at[:, columns(m, k)], send_sem=p_send.at[k, m],
            recv_sem=p_recv.at[k, m], device_id={"section": before}, device_id_type=MESH,
        )

    @pl.loop(0, steps * n)
    def _(i):
        k, o = i // n, lax.rem(i, n)
        d = lax.rem(me + 1 + o, n)
        cols = columns(d, k)
        mixed = (gk_ref[:, cols].astype(F32) * vi_ref[:, cols].astype(F32)).astype(BF16)
        pulled = (gq_ref[:, cols].astype(F32) * go_ref[:, cols].astype(F32)).astype(BF16)
        envelope = jnp.exp(-rate_ref[:, cols] * here(0, rows))
        filt = (fr_ref[:, cols].astype(F32) * envelope).astype(BF16)
        sbuf[k, d, :, 0:chunk] = mixed
        sbuf[k, d, :, chunk:2 * chunk] = filt
        sbuf[k, d, :, 2 * chunk:3 * chunk] = pulled

        @pl.when(o < n - 1)
        def _():
            send_in(k, d).start()

        @pl.when(o == n - 1)
        def _():
            rbuf[k, me, :, 0:chunk] = mixed
            rbuf[k, me, :, chunk:2 * chunk] = filt
            rbuf[k, me, :, 2 * chunk:3 * chunk] = pulled

    @pl.when(sec == nsec - 1)
    def _():
        op_ref[...] = jnp.zeros_like(op_ref)

    tile = 16
    top = lax.broadcasted_iota(jnp.int32, (rows, 1), 0)

    @pl.loop(0, steps)
    def _(k):
        @pl.loop(0, n - 1)
        def _(o):
            got_in(k, lax.rem(me + 1 + o, n)).wait_recv()

        @pl.loop(0, rows // tile)
        def _(t):
            at = pl.ds(pl.multiple_of(t * tile, tile), tile)
            low = pl.ds(pl.multiple_of(rows + t * tile, tile), tile)
            for g in range(3):
                lanes = slice(g * chunk, (g + 1) * chunk)
                x = [rbuf[k, m, at, lanes].astype(F32) for m in range(n)]
                zero = jnp.zeros_like(x[0])
                even = combine([(1.0, x[m]) for m in range(0, n, 2)], zero)
                odd = combine([(1.0, x[m]) for m in range(1, n, 2)], zero)
                part[0, at, lanes] = (even + odd).astype(BF16)
                part[0, low, lanes] = (even - odd).astype(BF16)
                for a in range(1, n // 2 + 1):
                    cos = [math.cos(math.pi * m * a / n) for m in range(n)]
                    sin = [math.sin(math.pi * m * a / n) for m in range(n)]
                    ce = combine([(cos[m], x[m]) for m in range(0, n, 2)], zero)
                    co = combine([(cos[m], x[m]) for m in range(1, n, 2)], zero)
                    se = combine([(sin[m], x[m]) for m in range(0, n, 2)], zero)
                    so = combine([(sin[m], x[m]) for m in range(1, n, 2)], zero)
                    part[a, at, lanes] = (ce + co).astype(BF16)
                    part[a, low, lanes] = (-se - so).astype(BF16)
                    if n - a != a:
                        part[n - a, at, lanes] = (ce - co).astype(BF16)
                        part[n - a, low, lanes] = (se - so).astype(BF16)

        @pl.loop(0, n)
        def _(a):
            spec = jnp.dot(fwd_ref[a], part[a], preferred_element_type=F32)
            mr, fr, pr = (spec[:rows, g * chunk:(g + 1) * chunk] for g in range(3))
            mi, fi, pi = (spec[rows:, g * chunk:(g + 1) * chunk] for g in range(3))
            real_pair = jnp.logical_and(top == 0, a == 0)

            def product(ar, ai, br, bi, sign):
                cross = ai * bi
                re = ar * br + jnp.where(real_pair, 0.0, sign * cross)
                im = jnp.where(real_pair, cross, ar * bi - sign * ai * br)
                return re, im

            outs = (
                product(fr, fi, mr, mi, -1.0),
                product(fr, fi, pr, pi, 1.0),
                product(mr, mi, pr, pi, 1.0),
            )
            for g in range(3):
                lanes = slice(g * chunk, (g + 1) * chunk)
                part[a, 0:rows, lanes] = outs[g][0].astype(BF16)
                part[a, rows:2 * rows, lanes] = outs[g][1].astype(BF16)
            fold[a] = jnp.dot(inv_ref[a], part[a], preferred_element_type=F32)

        def unfold(t, carry):
            rate_sum, skip_sum = carry
            at = pl.ds(pl.multiple_of(t * tile, tile), tile)
            low = pl.ds(pl.multiple_of(rows + t * tile, tile), tile)
            for g in range(3):
                lanes = slice(g * chunk, (g + 1) * chunk)
                re = [fold[a, at, lanes] for a in range(n)]
                im = [fold[a, low, lanes] for a in range(n)]
                zero = jnp.zeros_like(re[0])
                for m in range(n):
                    terms = [(1.0, re[0]), ((-1.0) ** m, im[0])]
                    for a in range(1, n):
                        terms.append((math.cos(math.pi * m * a / n), re[a]))
                        terms.append((-math.sin(math.pi * m * a / n), im[a]))
                    value = combine(terms, zero).astype(BF16)
                    obuf[k, m, at, lanes] = value
                    if g == 2:
                        when = lax.broadcasted_iota(jnp.int32, (tile, 1), 0) + (t * tile + m * rows)
                        when = when.astype(F32) * np.float32(1.0 / seq)
                        mixed = rbuf[k, m, at, 0:chunk].astype(F32)
                        filt = rbuf[k, m, at, chunk:2 * chunk].astype(F32)
                        pulled = rbuf[k, m, at, 2 * chunk:3 * chunk].astype(F32)
                        rate_sum = rate_sum + when * value.astype(F32) * filt
                        skip_sum = skip_sum + mixed * pulled
            return rate_sum, skip_sum

        start = jnp.zeros((tile, chunk), F32)
        rate_sum, skip_sum = lax.fori_loop(0, rows // tile, unfold, (start, start))
        mine = pl.ds(pl.multiple_of(k * chunk, chunk), chunk)
        sstat[0:1, mine] = -jnp.sum(rate_sum, axis=0, keepdims=True)
        sstat[1:2, mine] = jnp.sum(skip_sum, axis=0, keepdims=True)

        @pl.loop(0, n - 1)
        def _(o):
            send_out(k, lax.rem(me + 1 + o, n)).start()

        hbuf[k, me] = obuf[k, me]

    for o in range(1, n):
        send_stat(lax.rem(me + o, n)).start()
    gstat[me] = sstat[...]

    @pl.loop(0, steps * n)
    def _(i):
        k, o = i // n, lax.rem(i, n)
        m = lax.rem(me + o, n)

        @pl.when(o > 0)
        def _():
            got_out(k, m).wait_recv()

        cols = columns(m, k)
        conv = hbuf[k, m, :, 0:chunk].astype(F32)
        adjoint = hbuf[k, m, :, chunk:2 * chunk].astype(F32)
        corr = hbuf[k, m, :, 2 * chunk:3 * chunk].astype(F32)
        mixed = sbuf[k, m, :, 0:chunk].astype(F32)
        pulled = sbuf[k, m, :, 2 * chunk:3 * chunk].astype(F32)
        skip = skip_ref[:, cols]
        oq_ref[:, cols] = (go_ref[:, cols].astype(F32) * (conv + skip * mixed)).astype(BF16)
        mixed_grad = adjoint + skip * pulled
        pbuf[k, m] = (mixed_grad * gk_ref[:, cols].astype(F32)).astype(BF16)

        @pl.when(sec > 0)
        def _():
            pass_copy(k, m).start()

        ok_ref[:, cols] = (mixed_grad * vi_ref[:, cols].astype(F32)).astype(BF16)
        envelope = jnp.exp(-rate_ref[:, cols] * here(0, rows))
        of_ref[:, cols] = (corr * envelope).astype(BF16)

    for o in range(1, n):
        got_stat(lax.rem(me + o, n)).wait_recv()
    for m in range(n):
        orate_ref[:, m * width:(m + 1) * width] = gstat[m, 0:1, :]
        oskip_ref[:, m * width:(m + 1) * width] = gstat[m, 1:2, :]

    for o in range(1, n):
        send_stat(lax.rem(me + o, n)).wait_send()

    @pl.loop(0, steps * (n - 1))
    def _(i):
        k, o = i // (n - 1), lax.rem(i, n - 1)
        d = lax.rem(me + 1 + o, n)
        send_in(k, d).wait_send()
        send_out(k, d).wait_send()

    @pl.loop(0, steps * n)
    def _(i):
        k, m = i // n, lax.rem(i, n)

        @pl.when(sec > 0)
        def _():
            pass_copy(k, m).wait_send()

        @pl.when(sec < nsec - 1)
        def _():
            pass_copy(k, m).wait_recv()


def shards(n, nsec, gate_q, gate_k, value_in, filter_raw, decay_rate, skip_gain, grad_out):
    rows, channels = gate_q.shape[1:]
    width = channels // n
    chunk = 128
    steps = width // chunk
    fwd, inv = make_tables(n, rows)
    fwd, inv = jnp.asarray(fwd, BF16), jnp.asarray(inv, BF16)
    block = jax.ShapeDtypeStruct((rows, channels), BF16)
    row = jax.ShapeDtypeStruct((1, channels), F32)
    vmem = pl.BlockSpec(memory_space=pltpu.VMEM)
    message = (steps, n, rows, 3 * chunk)
    dma = pltpu.SemaphoreType.DMA
    outs = pl.pallas_call(
        functools.partial(kernel, n, nsec, chunk, steps),
        out_shape=(block, block, block, block, row, row),
        in_specs=[vmem] * 9,
        out_specs=(vmem,) * 6,
        scratch_shapes=[
            pltpu.VMEM(message, BF16),
            pltpu.VMEM(message, BF16),
            pltpu.VMEM(message, BF16),
            pltpu.VMEM(message, BF16),
            pltpu.VMEM((steps, n, rows, chunk), BF16),
            pltpu.VMEM((n, 2 * rows, 3 * chunk), BF16),
            pltpu.VMEM((n, 2 * rows, 3 * chunk), F32),
            pltpu.VMEM((2, width), F32),
            pltpu.VMEM((n, 2, width), F32),
            dma((steps, n)), dma((steps, n)), dma((steps, n)), dma((steps, n)),
            dma((steps, n)), dma((steps, n)), dma((n,)), dma((n,)),
        ],
        compiler_params=pltpu.CompilerParams(
            collective_id=0, has_side_effects=True, vmem_limit_bytes=50 * 1024 * 1024
        ),
        name="hyena_backward",
    )(
        gate_q[0], gate_k[0], value_in[0], filter_raw[0], grad_out[0],
        decay_rate, skip_gain, fwd, inv,
    )
    oq, ok, op, of, orate, oskip = outs
    return oq[None], ok[None], op[None], of[None], orate, oskip


def solution(mesh):
    n, nsec = mesh.shape["ctx"], mesh.shape["section"]
    tokens = P("section", "ctx", None)
    return jax.shard_map(
        functools.partial(shards, n, nsec),
        mesh=mesh,
        in_specs=(tokens, tokens, tokens, tokens, P("section", None), P("section", None), tokens),
        out_specs=(tokens, tokens, tokens, tokens, P("section", None), P("section", None)),
        check_vma=False,
    )
```

```python
import functools
import math

import jax
import jax.numpy as jnp
import numpy as np
from jax import lax
from jax.experimental import pallas as pl
from jax.experimental.pallas import tpu as pltpu
from jax.sharding import PartitionSpec as P

MESH = pl.DeviceIdType.MESH
F32 = jnp.float32
BF16 = jnp.bfloat16


def make_tables(n, rows):
    length = 2 * n * rows
    half = rows // 2
    j = np.arange(rows)[None, :]
    b = np.arange(rows)[:, None]

    def angle(a):
        return 2.0 * np.pi * ((j * (a + 2 * n * b)) % length) / length

    fwd = np.zeros((n, 2 * rows, 2 * rows))
    inv = np.zeros((n, 2 * rows, 2 * rows))
    for a in range(1, n):
        c, s = np.cos(angle(a)), np.sin(angle(a))
        fwd[a] = np.block([[c, s], [-s, c]])
        inv[a] = np.block([[c.T, -s.T], [s.T, c.T]]) * (2.0 / length)
    for slot, a in ((0, 0), (1, n)):
        c, s = np.cos(angle(a))[:half], np.sin(angle(a))[:half]
        weight = np.full((half, 1), 2.0 / length)
        re_rows = slice(slot * half, (slot + 1) * half)
        im_rows = slice(rows + slot * half, rows + (slot + 1) * half)
        cols = slice(slot * rows, (slot + 1) * rows)
        im = -s
        if slot == 0:
            im = im.copy()
            im[0] = np.cos(np.pi * np.arange(rows))
            weight[0] = 1.0 / length
        fwd[0, re_rows, cols] = c
        fwd[0, im_rows, cols] = im
        inv[0, cols, re_rows] = (c * weight).T
        inv[0, cols, im_rows] = (im * weight).T
    return fwd, inv


def scaled(coef, x):
    if abs(coef - 1.0) < 1e-12:
        return x
    if abs(coef + 1.0) < 1e-12:
        return -x
    return x * np.float32(coef)


def combine(terms, zero):
    total = None
    for coef, x in terms:
        if abs(coef) < 1e-12:
            continue
        if total is None:
            total = scaled(coef, x)
        elif coef < 0:
            total = total - scaled(-coef, x)
        else:
            total = total + scaled(coef, x)
    return zero if total is None else total


def kernel(
    n, nsec, chunk, steps,
    gq_hbm, gk_hbm, vi_hbm, fr_hbm, go_hbm, rate_hbm, skip_hbm, fwd_hbm, inv_hbm,
    oq_hbm, ok_hbm, op_ref, of_hbm, orate_hbm, oskip_hbm,
    gq_ref, gk_ref, vi_ref, fr_ref, go_ref, rate_ref, skip_ref, fwd_ref, inv_ref,
    ostage, zeros, orate_ref, oskip_ref, in_sem, row_sem, out_sem, end_sem,
    sbuf, rbuf, obuf, hbuf, pbuf, part, fold, sstat, gstat,
    s_send, s_recv, o_send, o_recv, p_send, p_recv, t_send, t_recv,
):
    rows = gq_ref.shape[0]
    width = chunk * steps
    seq = rows * n
    me = lax.axis_index("ctx")
    sec = lax.axis_index("section")
    before = lax.rem(sec + nsec - 1, nsec)
    after = lax.rem(sec + 1, nsec)

    def columns(owner, k):
        return pl.ds(pl.multiple_of(owner * width + k * chunk, chunk), chunk)

    tokens = (
        (gk_hbm, gk_ref), (vi_hbm, vi_ref), (gq_hbm, gq_ref), (go_hbm, go_ref), (fr_hbm, fr_ref)
    )
    whole = (
        (rate_hbm, rate_ref), (skip_hbm, skip_ref), (fwd_hbm, fwd_ref), (inv_hbm, inv_ref)
    )

    def load_first(g, d):
        hbm, ref = tokens[g]
        return pltpu.make_async_copy(
            hbm.at[:, columns(d, 0)], ref.at[:, columns(d, 0)], in_sem.at[g, 0, d]
        )

    def load_rest(g, d):
        hbm, ref = tokens[g]
        cols = pl.ds(pl.multiple_of(d * width + chunk, chunk), width - chunk)
        return pltpu.make_async_copy(hbm.at[:, cols], ref.at[:, cols], in_sem.at[g, 1, d])

    def load_whole(g):
        return pltpu.make_async_copy(whole[g][0], whole[g][1], row_sem.at[g])

    load_whole(0).start()
    for o in range(n):
        for g in range(5):
            load_first(g, lax.rem(me + 1 + o, n)).start()
    if steps > 1:
        for d in range(n):
            for g in range(5):
                load_rest(g, d).start()
    for g in range(1, 4):
        load_whole(g).start()

    barrier = pltpu.get_barrier_semaphore()
    for o in range(1, n):
        pl.semaphore_signal(
            barrier, inc=1, device_id={"ctx": lax.rem(me + o, n)}, device_id_type=MESH
        )
    for other in (before, after):
        pl.semaphore_signal(barrier, inc=1, device_id={"section": other}, device_id_type=MESH)
    pl.semaphore_wait(barrier, n + 1)
    load_whole(0).wait()

    def here(row0, count):
        row = lax.broadcasted_iota(jnp.int32, (count, 1), 0) + (row0 + me * rows)
        return row.astype(F32) * np.float32(1.0 / seq)

    def send_in(k, d):
        return pltpu.make_async_remote_copy(
            src_ref=sbuf.at[k, d], dst_ref=rbuf.at[k, me], send_sem=s_send.at[k, d],
            recv_sem=s_recv.at[k, me], device_id={"ctx": d}, device_id_type=MESH,
        )

    def got_in(k, m):
        return pltpu.make_async_remote_copy(
            src_ref=sbuf.at[k, m], dst_ref=rbuf.at[k, m], send_sem=s_send.at[k, m],
            recv_sem=s_recv.at[k, m], device_id={"ctx": m}, device_id_type=MESH,
        )

    def send_out(k, m):
        return pltpu.make_async_remote_copy(
            src_ref=obuf.at[k, m], dst_ref=hbuf.at[k, me], send_sem=o_send.at[k, m],
            recv_sem=o_recv.at[k, me], device_id={"ctx": m}, device_id_type=MESH,
        )

    def got_out(k, m):
        return pltpu.make_async_remote_copy(
            src_ref=obuf.at[k, m], dst_ref=hbuf.at[k, m], send_sem=o_send.at[k, m],
            recv_sem=o_recv.at[k, m], device_id={"ctx": m}, device_id_type=MESH,
        )

    def send_stat(d):
        return pltpu.make_async_remote_copy(
            src_ref=sstat, dst_ref=gstat.at[me], send_sem=t_send.at[d],
            recv_sem=t_recv.at[me], device_id={"ctx": d}, device_id_type=MESH,
        )

    def got_stat(m):
        return pltpu.make_async_remote_copy(
            src_ref=sstat, dst_ref=gstat.at[m], send_sem=t_send.at[m],
            recv_sem=t_recv.at[m], device_id={"ctx": m}, device_id_type=MESH,
        )

    def pass_copy(k, m):
        return pltpu.make_async_remote_copy(
            src_ref=pbuf.at[k, m], dst_ref=op_ref.at[:, columns(m, k)], send_sem=p_send.at[k, m],
            recv_sem=p_recv.at[k, m], device_id={"section": before}, device_id_type=MESH,
        )

    @pl.loop(0, steps * n)
    def _(i):
        k, o = i // n, lax.rem(i, n)
        d = lax.rem(me + 1 + o, n)
        cols = columns(d, k)

        @pl.when(k == 0)
        def _():
            for g in range(5):
                load_first(g, d).wait()

        if steps > 1:
            @pl.when(k == 1)
            def _():
                for g in range(5):
                    load_rest(g, d).wait()

        mixed = (gk_ref[:, cols].astype(F32) * vi_ref[:, cols].astype(F32)).astype(BF16)
        pulled = (gq_ref[:, cols].astype(F32) * go_ref[:, cols].astype(F32)).astype(BF16)
        envelope = jnp.exp(-rate_ref[:, cols] * here(0, rows))
        filt = (fr_ref[:, cols].astype(F32) * envelope).astype(BF16)
        sbuf[k, d, :, 0:chunk] = mixed
        sbuf[k, d, :, chunk:2 * chunk] = filt
        sbuf[k, d, :, 2 * chunk:3 * chunk] = pulled

        @pl.when(o < n - 1)
        def _():
            send_in(k, d).start()

        @pl.when(o == n - 1)
        def _():
            rbuf[k, me, :, 0:chunk] = mixed
            rbuf[k, me, :, chunk:2 * chunk] = filt
            rbuf[k, me, :, 2 * chunk:3 * chunk] = pulled

    def clear():
        return pltpu.make_async_copy(zeros, op_ref, end_sem.at[0])

    @pl.when(sec == nsec - 1)
    def _():
        zeros[...] = jnp.zeros_like(zeros)
        clear().start()

    for g in range(1, 4):
        load_whole(g).wait()

    def store(g, k, m):
        out = (oq_hbm, ok_hbm, of_hbm)[g]
        return pltpu.make_async_copy(
            ostage.at[g, k, m], out.at[:, columns(m, k)], out_sem.at[g, k, m]
        )

    tile = 16
    top = lax.broadcasted_iota(jnp.int32, (rows, 1), 0)

    @pl.loop(0, steps)
    def _(k):
        @pl.loop(0, n - 1)
        def _(o):
            got_in(k, lax.rem(me + 1 + o, n)).wait_recv()

        @pl.loop(0, rows // tile)
        def _(t):
            at = pl.ds(pl.multiple_of(t * tile, tile), tile)
            low = pl.ds(pl.multiple_of(rows + t * tile, tile), tile)
            for g in range(3):
                lanes = slice(g * chunk, (g + 1) * chunk)
                x = [rbuf[k, m, at, lanes].astype(F32) for m in range(n)]
                zero = jnp.zeros_like(x[0])
                even = combine([(1.0, x[m]) for m in range(0, n, 2)], zero)
                odd = combine([(1.0, x[m]) for m in range(1, n, 2)], zero)
                part[0, at, lanes] = (even + odd).astype(BF16)
                part[0, low, lanes] = (even - odd).astype(BF16)
                for a in range(1, n // 2 + 1):
                    cos = [math.cos(math.pi * m * a / n) for m in range(n)]
                    sin = [math.sin(math.pi * m * a / n) for m in range(n)]
                    ce = combine([(cos[m], x[m]) for m in range(0, n, 2)], zero)
                    co = combine([(cos[m], x[m]) for m in range(1, n, 2)], zero)
                    se = combine([(sin[m], x[m]) for m in range(0, n, 2)], zero)
                    so = combine([(sin[m], x[m]) for m in range(1, n, 2)], zero)
                    part[a, at, lanes] = (ce + co).astype(BF16)
                    part[a, low, lanes] = (-se - so).astype(BF16)
                    if n - a != a:
                        part[n - a, at, lanes] = (ce - co).astype(BF16)
                        part[n - a, low, lanes] = (se - so).astype(BF16)

        @pl.loop(0, n)
        def _(a):
            spec = jnp.dot(fwd_ref[a], part[a], preferred_element_type=F32)
            mr, fr, pr = (spec[:rows, g * chunk:(g + 1) * chunk] for g in range(3))
            mi, fi, pi = (spec[rows:, g * chunk:(g + 1) * chunk] for g in range(3))
            real_pair = jnp.logical_and(top == 0, a == 0)

            def product(ar, ai, br, bi, sign):
                cross = ai * bi
                re = ar * br + jnp.where(real_pair, 0.0, sign * cross)
                im = jnp.where(real_pair, cross, ar * bi - sign * ai * br)
                return re, im

            outs = (
                product(fr, fi, mr, mi, -1.0),
                product(fr, fi, pr, pi, 1.0),
                product(mr, mi, pr, pi, 1.0),
            )
            for g in range(3):
                lanes = slice(g * chunk, (g + 1) * chunk)
                part[a, 0:rows, lanes] = outs[g][0].astype(BF16)
                part[a, rows:2 * rows, lanes] = outs[g][1].astype(BF16)
            fold[a] = jnp.dot(inv_ref[a], part[a], preferred_element_type=F32)

        def unfold(t, carry):
            rate_sum, skip_sum = carry
            at = pl.ds(pl.multiple_of(t * tile, tile), tile)
            low = pl.ds(pl.multiple_of(rows + t * tile, tile), tile)
            for g in range(3):
                lanes = slice(g * chunk, (g + 1) * chunk)
                re = [fold[a, at, lanes] for a in range(n)]
                im = [fold[a, low, lanes] for a in range(n)]
                zero = jnp.zeros_like(re[0])
                for m in range(n):
                    terms = [(1.0, re[0]), ((-1.0) ** m, im[0])]
                    for a in range(1, n):
                        terms.append((math.cos(math.pi * m * a / n), re[a]))
                        terms.append((-math.sin(math.pi * m * a / n), im[a]))
                    value = combine(terms, zero).astype(BF16)
                    obuf[k, m, at, lanes] = value
                    if g == 2:
                        when = lax.broadcasted_iota(jnp.int32, (tile, 1), 0) + (t * tile + m * rows)
                        when = when.astype(F32) * np.float32(1.0 / seq)
                        mixed = rbuf[k, m, at, 0:chunk].astype(F32)
                        filt = rbuf[k, m, at, chunk:2 * chunk].astype(F32)
                        pulled = rbuf[k, m, at, 2 * chunk:3 * chunk].astype(F32)
                        rate_sum = rate_sum + when * value.astype(F32) * filt
                        skip_sum = skip_sum + mixed * pulled
            return rate_sum, skip_sum

        start = jnp.zeros((tile, chunk), F32)
        rate_sum, skip_sum = lax.fori_loop(0, rows // tile, unfold, (start, start))
        mine = pl.ds(pl.multiple_of(k * chunk, chunk), chunk)
        sstat[0:1, mine] = -jnp.sum(rate_sum, axis=0, keepdims=True)
        sstat[1:2, mine] = jnp.sum(skip_sum, axis=0, keepdims=True)

        @pl.loop(0, n - 1)
        def _(o):
            send_out(k, lax.rem(me + 1 + o, n)).start()

        hbuf[k, me] = obuf[k, me]

    for o in range(1, n):
        send_stat(lax.rem(me + o, n)).start()
    gstat[me] = sstat[...]

    @pl.loop(0, steps * n)
    def _(i):
        k, o = i // n, lax.rem(i, n)
        m = lax.rem(me + o, n)

        @pl.when(o > 0)
        def _():
            got_out(k, m).wait_recv()

        cols = columns(m, k)
        conv = hbuf[k, m, :, 0:chunk].astype(F32)
        adjoint = hbuf[k, m, :, chunk:2 * chunk].astype(F32)
        corr = hbuf[k, m, :, 2 * chunk:3 * chunk].astype(F32)
        mixed = sbuf[k, m, :, 0:chunk].astype(F32)
        pulled = sbuf[k, m, :, 2 * chunk:3 * chunk].astype(F32)
        skip = skip_ref[:, cols]
        ostage[0, k, m] = (go_ref[:, cols].astype(F32) * (conv + skip * mixed)).astype(BF16)
        mixed_grad = adjoint + skip * pulled
        pbuf[k, m] = (mixed_grad * gk_ref[:, cols].astype(F32)).astype(BF16)

        @pl.when(sec > 0)
        def _():
            pass_copy(k, m).start()

        store(0, k, m).start()
        ostage[1, k, m] = (mixed_grad * vi_ref[:, cols].astype(F32)).astype(BF16)
        store(1, k, m).start()
        envelope = jnp.exp(-rate_ref[:, cols] * here(0, rows))
        ostage[2, k, m] = (corr * envelope).astype(BF16)
        store(2, k, m).start()

    for o in range(1, n):
        got_stat(lax.rem(me + o, n)).wait_recv()
    for m in range(n):
        orate_ref[:, m * width:(m + 1) * width] = gstat[m, 0:1, :]
        oskip_ref[:, m * width:(m + 1) * width] = gstat[m, 1:2, :]
    rows_out = (
        pltpu.make_async_copy(orate_ref, orate_hbm, end_sem.at[1]),
        pltpu.make_async_copy(oskip_ref, oskip_hbm, end_sem.at[2]),
    )
    for copy in rows_out:
        copy.start()

    for o in range(1, n):
        send_stat(lax.rem(me + o, n)).wait_send()

    @pl.loop(0, steps * (n - 1))
    def _(i):
        k, o = i // (n - 1), lax.rem(i, n - 1)
        d = lax.rem(me + 1 + o, n)
        send_in(k, d).wait_send()
        send_out(k, d).wait_send()

    @pl.loop(0, steps * n)
    def _(i):
        k, m = i // n, lax.rem(i, n)

        @pl.when(sec > 0)
        def _():
            pass_copy(k, m).wait_send()

        @pl.when(sec < nsec - 1)
        def _():
            pass_copy(k, m).wait_recv()

        for g in range(3):
            store(g, k, m).wait()

    for copy in rows_out:
        copy.wait()

    @pl.when(sec == nsec - 1)
    def _():
        clear().wait()


def finish(pieces, *refs):
    count = len(refs) // 2
    sem = refs[-1]
    copies = []
    for g in range(count):
        src, dst = refs[g], refs[count + g]
        parts = pieces if src.shape[0] % pieces == 0 else 1
        size = src.shape[0] // parts
        for p in range(parts):
            at = pl.ds(p * size, size)
            copies.append(pltpu.make_async_copy(src.at[at], dst.at[at], sem.at[g, p]))
    for copy in copies:
        copy.start()
    for copy in copies:
        copy.wait()


def shards(n, nsec, gate_q, gate_k, value_in, filter_raw, decay_rate, skip_gain, grad_out):
    rows, channels = gate_q.shape[1:]
    width = channels // n
    chunk = 128
    steps = width // chunk
    fwd, inv = make_tables(n, rows)
    fwd, inv = jnp.asarray(fwd, BF16), jnp.asarray(inv, BF16)
    block = jax.ShapeDtypeStruct((rows, channels), BF16)
    row = jax.ShapeDtypeStruct((1, channels), F32)
    message = (steps, n, rows, 3 * chunk)
    dma = pltpu.SemaphoreType.DMA
    anywhere = pl.BlockSpec(memory_space=pl.ANY)
    shapes = (block, block, block, block, row, row)
    outs = pl.pallas_call(
        functools.partial(kernel, n, nsec, chunk, steps),
        out_shape=shapes,
        in_specs=[anywhere] * 9,
        out_specs=(anywhere,) * 6,
        scratch_shapes=[
            *([pltpu.VMEM((rows, channels), BF16)] * 5),
            *([pltpu.VMEM((1, channels), F32)] * 2),
            *([pltpu.VMEM(fwd.shape, BF16)] * 2),
            pltpu.VMEM((3, steps, n, rows, chunk), BF16),
            pltpu.VMEM((rows, channels), BF16),
            *([pltpu.VMEM((1, channels), F32)] * 2),
            dma((5, 2, n)), dma((4,)), dma((3, steps, n)), dma((3,)),
            pltpu.VMEM(message, BF16),
            pltpu.VMEM(message, BF16),
            pltpu.VMEM(message, BF16),
            pltpu.VMEM(message, BF16),
            pltpu.VMEM((steps, n, rows, chunk), BF16),
            pltpu.VMEM((n, 2 * rows, 3 * chunk), BF16),
            pltpu.VMEM((n, 2 * rows, 3 * chunk), F32),
            pltpu.VMEM((2, width), F32),
            pltpu.VMEM((n, 2, width), F32),
            dma((steps, n)), dma((steps, n)), dma((steps, n)), dma((steps, n)),
            dma((steps, n)), dma((steps, n)), dma((n,)), dma((n,)),
        ],
        compiler_params=pltpu.CompilerParams(
            collective_id=0, has_side_effects=True, vmem_limit_bytes=58 * 1024 * 1024
        ),
        name="hyena_backward",
    )(
        gate_q[0], gate_k[0], value_in[0], filter_raw[0], grad_out[0],
        decay_rate, skip_gain, fwd, inv,
    )
    pieces = 4
    oq, ok, op, of, orate, oskip = pl.pallas_call(
        functools.partial(finish, pieces),
        out_shape=shapes,
        in_specs=[anywhere] * 6,
        out_specs=(anywhere,) * 6,
        scratch_shapes=[dma((6, pieces))],
        name="hand_over",
    )(*outs)
    return oq[None], ok[None], op[None], of[None], orate, oskip


def solution(mesh):
    n, nsec = mesh.shape["ctx"], mesh.shape["section"]
    tokens = P("section", "ctx", None)
    return jax.shard_map(
        functools.partial(shards, n, nsec),
        mesh=mesh,
        in_specs=(tokens, tokens, tokens, tokens, P("section", None), P("section", None), tokens),
        out_specs=(tokens, tokens, tokens, tokens, P("section", None), P("section", None)),
        check_vma=False,
    )
```

```python
import functools
import math

import jax
import jax.numpy as jnp
import numpy as np
from jax import lax
from jax.experimental import pallas as pl
from jax.experimental.pallas import tpu as pltpu
from jax.sharding import PartitionSpec as P

MESH = pl.DeviceIdType.MESH
F32 = jnp.float32
BF16 = jnp.bfloat16


def make_tables(n, rows):
    length = 2 * n * rows
    half = rows // 2
    j = np.arange(rows)[None, :]
    b = np.arange(rows)[:, None]

    def angle(a):
        return 2.0 * np.pi * ((j * (a + 2 * n * b)) % length) / length

    fwd = np.zeros((n, 2 * rows, 2 * rows))
    inv = np.zeros((n, 2 * rows, 2 * rows))
    for a in range(1, n):
        c, s = np.cos(angle(a)), np.sin(angle(a))
        fwd[a] = np.block([[c, s], [-s, c]])
        inv[a] = np.block([[c.T, -s.T], [s.T, c.T]]) * (2.0 / length)
    for slot, a in ((0, 0), (1, n)):
        c, s = np.cos(angle(a))[:half], np.sin(angle(a))[:half]
        weight = np.full((half, 1), 2.0 / length)
        re_rows = slice(slot * half, (slot + 1) * half)
        im_rows = slice(rows + slot * half, rows + (slot + 1) * half)
        cols = slice(slot * rows, (slot + 1) * rows)
        im = -s
        if slot == 0:
            im = im.copy()
            im[0] = np.cos(np.pi * np.arange(rows))
            weight[0] = 1.0 / length
        fwd[0, re_rows, cols] = c
        fwd[0, im_rows, cols] = im
        inv[0, cols, re_rows] = (c * weight).T
        inv[0, cols, im_rows] = (im * weight).T
    return fwd, inv


def scaled(coef, x):
    if abs(coef - 1.0) < 1e-12:
        return x
    if abs(coef + 1.0) < 1e-12:
        return -x
    return x * np.float32(coef)


def combine(terms, zero):
    total = None
    for coef, x in terms:
        if abs(coef) < 1e-12:
            continue
        if total is None:
            total = scaled(coef, x)
        elif coef < 0:
            total = total - scaled(-coef, x)
        else:
            total = total + scaled(coef, x)
    return zero if total is None else total


def kernel(
    n, nsec, chunk, steps,
    gq_hbm, gk_hbm, vi_hbm, fr_hbm, go_hbm, rate_hbm, skip_hbm, fwd_hbm, inv_hbm,
    oq_hbm, ok_hbm, op_ref, of_hbm, orate_hbm, oskip_hbm,
    gq_ref, gk_ref, vi_ref, fr_ref, go_ref, rate_ref, skip_ref, fwd_ref, inv_ref,
    ostage, zeros, orate_ref, oskip_ref, in_sem, row_sem, out_sem, end_sem,
    sbuf, rbuf, obuf, hbuf, pbuf, part, fold, sstat, gstat,
    s_send, s_recv, o_send, o_recv, p_send, p_recv, t_send, t_recv,
):
    rows = gq_ref.shape[0]
    width = chunk * steps
    seq = rows * n
    me = lax.axis_index("ctx")
    sec = lax.axis_index("section")
    before = lax.rem(sec + nsec - 1, nsec)
    after = lax.rem(sec + 1, nsec)

    def columns(owner, k):
        return pl.ds(pl.multiple_of(owner * width + k * chunk, chunk), chunk)

    tokens = (
        (gk_hbm, gk_ref), (vi_hbm, vi_ref), (gq_hbm, gq_ref), (go_hbm, go_ref), (fr_hbm, fr_ref)
    )
    whole = (
        (rate_hbm, rate_ref), (skip_hbm, skip_ref), (fwd_hbm, fwd_ref), (inv_hbm, inv_ref)
    )

    def load_first(g, d):
        hbm, ref = tokens[g]
        return pltpu.make_async_copy(
            hbm.at[:, columns(d, 0)], ref.at[:, columns(d, 0)], in_sem.at[g, 0, d]
        )

    def load_rest(g, d):
        hbm, ref = tokens[g]
        cols = pl.ds(pl.multiple_of(d * width + chunk, chunk), width - chunk)
        return pltpu.make_async_copy(hbm.at[:, cols], ref.at[:, cols], in_sem.at[g, 1, d])

    def load_whole(g):
        return pltpu.make_async_copy(whole[g][0], whole[g][1], row_sem.at[g])

    load_whole(0).start()
    for o in range(n):
        for g in range(5):
            load_first(g, lax.rem(me + 1 + o, n)).start()
    if steps > 1:
        for d in range(n):
            for g in range(5):
                load_rest(g, d).start()
    for g in range(1, 4):
        load_whole(g).start()

    barrier = pltpu.get_barrier_semaphore()
    for o in range(1, n):
        pl.semaphore_signal(
            barrier, inc=1, device_id={"ctx": lax.rem(me + o, n)}, device_id_type=MESH
        )
    for other in (before, after):
        pl.semaphore_signal(barrier, inc=1, device_id={"section": other}, device_id_type=MESH)
    pl.semaphore_wait(barrier, n + 1)
    load_whole(0).wait()

    def here(row0, count):
        row = lax.broadcasted_iota(jnp.int32, (count, 1), 0) + (row0 + me * rows)
        return row.astype(F32) * np.float32(1.0 / seq)

    def send_in(k, d):
        return pltpu.make_async_remote_copy(
            src_ref=sbuf.at[k, d], dst_ref=rbuf.at[k, me], send_sem=s_send.at[k, d],
            recv_sem=s_recv.at[k, me], device_id={"ctx": d}, device_id_type=MESH,
        )

    def got_in(k, m):
        return pltpu.make_async_remote_copy(
            src_ref=sbuf.at[k, m], dst_ref=rbuf.at[k, m], send_sem=s_send.at[k, m],
            recv_sem=s_recv.at[k, m], device_id={"ctx": m}, device_id_type=MESH,
        )

    def send_out(k, m):
        return pltpu.make_async_remote_copy(
            src_ref=obuf.at[k, m], dst_ref=hbuf.at[k, me], send_sem=o_send.at[k, m],
            recv_sem=o_recv.at[k, me], device_id={"ctx": m}, device_id_type=MESH,
        )

    def got_out(k, m):
        return pltpu.make_async_remote_copy(
            src_ref=obuf.at[k, m], dst_ref=hbuf.at[k, m], send_sem=o_send.at[k, m],
            recv_sem=o_recv.at[k, m], device_id={"ctx": m}, device_id_type=MESH,
        )

    def send_stat(d):
        return pltpu.make_async_remote_copy(
            src_ref=sstat, dst_ref=gstat.at[me], send_sem=t_send.at[d],
            recv_sem=t_recv.at[me], device_id={"ctx": d}, device_id_type=MESH,
        )

    def got_stat(m):
        return pltpu.make_async_remote_copy(
            src_ref=sstat, dst_ref=gstat.at[m], send_sem=t_send.at[m],
            recv_sem=t_recv.at[m], device_id={"ctx": m}, device_id_type=MESH,
        )

    def pass_copy(k, m):
        return pltpu.make_async_remote_copy(
            src_ref=pbuf.at[k, m], dst_ref=op_ref.at[:, columns(m, k)], send_sem=p_send.at[k, m],
            recv_sem=p_recv.at[k, m], device_id={"section": before}, device_id_type=MESH,
        )

    @pl.loop(0, steps * n)
    def _(i):
        k, o = i // n, lax.rem(i, n)
        d = lax.rem(me + 1 + o, n)
        cols = columns(d, k)

        @pl.when(k == 0)
        def _():
            for g in range(5):
                load_first(g, d).wait()

        if steps > 1:
            @pl.when(k == 1)
            def _():
                for g in range(5):
                    load_rest(g, d).wait()

        mixed = (gk_ref[:, cols].astype(F32) * vi_ref[:, cols].astype(F32)).astype(BF16)
        pulled = (gq_ref[:, cols].astype(F32) * go_ref[:, cols].astype(F32)).astype(BF16)
        envelope = jnp.exp(-rate_ref[:, cols] * here(0, rows))
        filt = (fr_ref[:, cols].astype(F32) * envelope).astype(BF16)
        sbuf[k, d, :, 0:chunk] = mixed
        sbuf[k, d, :, chunk:2 * chunk] = filt
        sbuf[k, d, :, 2 * chunk:3 * chunk] = pulled

        @pl.when(o < n - 1)
        def _():
            send_in(k, d).start()

        @pl.when(o == n - 1)
        def _():
            rbuf[k, me, :, 0:chunk] = mixed
            rbuf[k, me, :, chunk:2 * chunk] = filt
            rbuf[k, me, :, 2 * chunk:3 * chunk] = pulled

    def clear():
        return pltpu.make_async_copy(zeros, op_ref, end_sem.at[0])

    @pl.when(sec == nsec - 1)
    def _():
        zeros[...] = jnp.zeros_like(zeros)
        clear().start()

    for g in range(1, 4):
        load_whole(g).wait()

    def store(g, k, m):
        out = (oq_hbm, ok_hbm, of_hbm)[g]
        return pltpu.make_async_copy(
            ostage.at[g, k, m], out.at[:, columns(m, k)], out_sem.at[g, k, m]
        )

    tile = 16
    top = lax.broadcasted_iota(jnp.int32, (rows, 1), 0)

    @pl.loop(0, steps)
    def _(k):
        @pl.loop(0, n - 1)
        def _(o):
            got_in(k, lax.rem(me + 1 + o, n)).wait_recv()

        @pl.loop(0, rows // tile)
        def _(t):
            at = pl.ds(pl.multiple_of(t * tile, tile), tile)
            low = pl.ds(pl.multiple_of(rows + t * tile, tile), tile)
            for g in range(3):
                lanes = slice(g * chunk, (g + 1) * chunk)
                x = [rbuf[k, m, at, lanes].astype(F32) for m in range(n)]
                zero = jnp.zeros_like(x[0])
                even = combine([(1.0, x[m]) for m in range(0, n, 2)], zero)
                odd = combine([(1.0, x[m]) for m in range(1, n, 2)], zero)
                part[0, at, lanes] = (even + odd).astype(BF16)
                part[0, low, lanes] = (even - odd).astype(BF16)
                for a in range(1, n // 2 + 1):
                    cos = [math.cos(math.pi * m * a / n) for m in range(n)]
                    sin = [math.sin(math.pi * m * a / n) for m in range(n)]
                    ce = combine([(cos[m], x[m]) for m in range(0, n, 2)], zero)
                    co = combine([(cos[m], x[m]) for m in range(1, n, 2)], zero)
                    se = combine([(sin[m], x[m]) for m in range(0, n, 2)], zero)
                    so = combine([(sin[m], x[m]) for m in range(1, n, 2)], zero)
                    part[a, at, lanes] = (ce + co).astype(BF16)
                    part[a, low, lanes] = (-se - so).astype(BF16)
                    if n - a != a:
                        part[n - a, at, lanes] = (ce - co).astype(BF16)
                        part[n - a, low, lanes] = (se - so).astype(BF16)

        @pl.loop(0, n)
        def _(a):
            spec = jnp.dot(fwd_ref[a], part[a], preferred_element_type=F32)
            mr, fr, pr = (spec[:rows, g * chunk:(g + 1) * chunk] for g in range(3))
            mi, fi, pi = (spec[rows:, g * chunk:(g + 1) * chunk] for g in range(3))
            real_pair = jnp.logical_and(top == 0, a == 0)

            def product(ar, ai, br, bi, sign):
                cross = ai * bi
                re = ar * br + jnp.where(real_pair, 0.0, sign * cross)
                im = jnp.where(real_pair, cross, ar * bi - sign * ai * br)
                return re, im

            outs = (
                product(fr, fi, mr, mi, -1.0),
                product(fr, fi, pr, pi, 1.0),
                product(mr, mi, pr, pi, 1.0),
            )
            for g in range(3):
                lanes = slice(g * chunk, (g + 1) * chunk)
                part[a, 0:rows, lanes] = outs[g][0].astype(BF16)
                part[a, rows:2 * rows, lanes] = outs[g][1].astype(BF16)
            fold[a] = jnp.dot(inv_ref[a], part[a], preferred_element_type=F32)

        def unfold(t, carry):
            rate_sum, skip_sum = carry
            at = pl.ds(pl.multiple_of(t * tile, tile), tile)
            low = pl.ds(pl.multiple_of(rows + t * tile, tile), tile)
            for g in range(3):
                lanes = slice(g * chunk, (g + 1) * chunk)
                re = [fold[a, at, lanes] for a in range(n)]
                im = [fold[a, low, lanes] for a in range(n)]
                zero = jnp.zeros_like(re[0])
                for m in range(n):
                    terms = [(1.0, re[0]), ((-1.0) ** m, im[0])]
                    for a in range(1, n):
                        terms.append((math.cos(math.pi * m * a / n), re[a]))
                        terms.append((-math.sin(math.pi * m * a / n), im[a]))
                    value = combine(terms, zero).astype(BF16)
                    obuf[k, m, at, lanes] = value
                    if g == 2:
                        when = lax.broadcasted_iota(jnp.int32, (tile, 1), 0) + (t * tile + m * rows)
                        when = when.astype(F32) * np.float32(1.0 / seq)
                        mixed = rbuf[k, m, at, 0:chunk].astype(F32)
                        filt = rbuf[k, m, at, chunk:2 * chunk].astype(F32)
                        pulled = rbuf[k, m, at, 2 * chunk:3 * chunk].astype(F32)
                        rate_sum = rate_sum + when * value.astype(F32) * filt
                        skip_sum = skip_sum + mixed * pulled
            return rate_sum, skip_sum

        start = jnp.zeros((tile, chunk), F32)
        rate_sum, skip_sum = lax.fori_loop(0, rows // tile, unfold, (start, start))
        mine = pl.ds(pl.multiple_of(k * chunk, chunk), chunk)
        sstat[0:1, mine] = -jnp.sum(rate_sum, axis=0, keepdims=True)
        sstat[1:2, mine] = jnp.sum(skip_sum, axis=0, keepdims=True)

        @pl.loop(0, n - 1)
        def _(o):
            send_out(k, lax.rem(me + 1 + o, n)).start()

        hbuf[k, me] = obuf[k, me]

    for o in range(1, n):
        send_stat(lax.rem(me + o, n)).start()
    gstat[me] = sstat[...]

    @pl.loop(0, steps * n)
    def _(i):
        k, o = i // n, lax.rem(i, n)
        m = lax.rem(me + o, n)

        @pl.when(o > 0)
        def _():
            got_out(k, m).wait_recv()

        cols = columns(m, k)
        conv = hbuf[k, m, :, 0:chunk].astype(F32)
        adjoint = hbuf[k, m, :, chunk:2 * chunk].astype(F32)
        corr = hbuf[k, m, :, 2 * chunk:3 * chunk].astype(F32)
        mixed = sbuf[k, m, :, 0:chunk].astype(F32)
        pulled = sbuf[k, m, :, 2 * chunk:3 * chunk].astype(F32)
        skip = skip_ref[:, cols]
        ostage[0, k, m] = (go_ref[:, cols].astype(F32) * (conv + skip * mixed)).astype(BF16)
        mixed_grad = adjoint + skip * pulled
        pbuf[k, m] = (mixed_grad * gk_ref[:, cols].astype(F32)).astype(BF16)

        @pl.when(sec > 0)
        def _():
            pass_copy(k, m).start()

        store(0, k, m).start()
        ostage[1, k, m] = (mixed_grad * vi_ref[:, cols].astype(F32)).astype(BF16)
        store(1, k, m).start()
        envelope = jnp.exp(-rate_ref[:, cols] * here(0, rows))
        ostage[2, k, m] = (corr * envelope).astype(BF16)
        store(2, k, m).start()

    for o in range(1, n):
        got_stat(lax.rem(me + o, n)).wait_recv()
    for m in range(n):
        orate_ref[:, m * width:(m + 1) * width] = gstat[m, 0:1, :]
        oskip_ref[:, m * width:(m + 1) * width] = gstat[m, 1:2, :]
    rows_out = (
        pltpu.make_async_copy(orate_ref, orate_hbm, end_sem.at[1]),
        pltpu.make_async_copy(oskip_ref, oskip_hbm, end_sem.at[2]),
    )
    for copy in rows_out:
        copy.start()

    for o in range(1, n):
        send_stat(lax.rem(me + o, n)).wait_send()

    @pl.loop(0, steps * (n - 1))
    def _(i):
        k, o = i // (n - 1), lax.rem(i, n - 1)
        d = lax.rem(me + 1 + o, n)
        send_in(k, d).wait_send()
        send_out(k, d).wait_send()

    @pl.loop(0, steps * n)
    def _(i):
        k, m = i // n, lax.rem(i, n)

        @pl.when(sec > 0)
        def _():
            pass_copy(k, m).wait_send()

        @pl.when(sec < nsec - 1)
        def _():
            pass_copy(k, m).wait_recv()

        for g in range(3):
            store(g, k, m).wait()

    for copy in rows_out:
        copy.wait()

    @pl.when(sec == nsec - 1)
    def _():
        clear().wait()


def finish(pieces, *refs):
    count = (len(refs) - 2) // 3
    load_sem, store_sem = refs[-2:]
    copies = []
    for g in range(count):
        src, dst, held = refs[g], refs[count + g], refs[2 * count + g]
        parts = pieces if src.shape[0] % pieces == 0 else 1
        size = src.shape[0] // parts
        for p in range(parts):
            at = pl.ds(p * size, size)
            copies.append((
                pltpu.make_async_copy(src.at[at], held.at[at], load_sem.at[g, p]),
                pltpu.make_async_copy(held.at[at], dst.at[at], store_sem.at[g, p]),
            ))
    for load, _ in copies:
        load.start()
    for load, store in copies:
        load.wait()
        store.start()
    for _, store in copies:
        store.wait()


def shards(n, nsec, gate_q, gate_k, value_in, filter_raw, decay_rate, skip_gain, grad_out):
    rows, channels = gate_q.shape[1:]
    width = channels // n
    chunk = 128
    steps = width // chunk
    fwd, inv = make_tables(n, rows)
    fwd, inv = jnp.asarray(fwd, BF16), jnp.asarray(inv, BF16)
    block = jax.ShapeDtypeStruct((rows, channels), BF16)
    row = jax.ShapeDtypeStruct((1, channels), F32)
    message = (steps, n, rows, 3 * chunk)
    dma = pltpu.SemaphoreType.DMA
    anywhere = pl.BlockSpec(memory_space=pl.ANY)
    shapes = (block, block, block, block, row, row)
    outs = pl.pallas_call(
        functools.partial(kernel, n, nsec, chunk, steps),
        out_shape=shapes,
        in_specs=[anywhere] * 9,
        out_specs=(anywhere,) * 6,
        scratch_shapes=[
            *([pltpu.VMEM((rows, channels), BF16)] * 5),
            *([pltpu.VMEM((1, channels), F32)] * 2),
            *([pltpu.VMEM(fwd.shape, BF16)] * 2),
            pltpu.VMEM((3, steps, n, rows, chunk), BF16),
            pltpu.VMEM((rows, channels), BF16),
            *([pltpu.VMEM((1, channels), F32)] * 2),
            dma((5, 2, n)), dma((4,)), dma((3, steps, n)), dma((3,)),
            pltpu.VMEM(message, BF16),
            pltpu.VMEM(message, BF16),
            pltpu.VMEM(message, BF16),
            pltpu.VMEM(message, BF16),
            pltpu.VMEM((steps, n, rows, chunk), BF16),
            pltpu.VMEM((n, 2 * rows, 3 * chunk), BF16),
            pltpu.VMEM((n, 2 * rows, 3 * chunk), F32),
            pltpu.VMEM((2, width), F32),
            pltpu.VMEM((n, 2, width), F32),
            dma((steps, n)), dma((steps, n)), dma((steps, n)), dma((steps, n)),
            dma((steps, n)), dma((steps, n)), dma((n,)), dma((n,)),
        ],
        compiler_params=pltpu.CompilerParams(
            collective_id=0, has_side_effects=True, vmem_limit_bytes=58 * 1024 * 1024
        ),
        name="hyena_backward",
    )(
        gate_q[0], gate_k[0], value_in[0], filter_raw[0], grad_out[0],
        decay_rate, skip_gain, fwd, inv,
    )
    pieces = 4
    oq, ok, op, of, orate, oskip = pl.pallas_call(
        functools.partial(finish, pieces),
        out_shape=shapes,
        in_specs=[anywhere] * 6,
        out_specs=(anywhere,) * 6,
        scratch_shapes=[
            *(pltpu.VMEM(shape.shape, shape.dtype) for shape in shapes),
            dma((6, pieces)), dma((6, pieces)),
        ],
        name="hand_over",
    )(*outs)
    return oq[None], ok[None], op[None], of[None], orate, oskip


def solution(mesh):
    n, nsec = mesh.shape["ctx"], mesh.shape["section"]
    tokens = P("section", "ctx", None)
    return jax.shard_map(
        functools.partial(shards, n, nsec),
        mesh=mesh,
        in_specs=(tokens, tokens, tokens, tokens, P("section", None), P("section", None), tokens),
        out_specs=(tokens, tokens, tokens, tokens, P("section", None), P("section", None)),
        check_vma=False,
    )
```

```python
import functools
import math

import jax
import jax.numpy as jnp
import numpy as np
from jax import lax
from jax.experimental import pallas as pl
from jax.experimental.pallas import tpu as pltpu
from jax.sharding import PartitionSpec as P

MESH = pl.DeviceIdType.MESH
F32 = jnp.float32
BF16 = jnp.bfloat16


def make_tables(n, rows):
    length = 2 * n * rows
    half = rows // 2
    j = np.arange(rows)[None, :]
    b = np.arange(rows)[:, None]

    def angle(a):
        return 2.0 * np.pi * ((j * (a + 2 * n * b)) % length) / length

    fwd = np.zeros((n, 2 * rows, 2 * rows))
    inv = np.zeros((n, 2 * rows, 2 * rows))
    for a in range(1, n):
        c, s = np.cos(angle(a)), np.sin(angle(a))
        fwd[a] = np.block([[c, s], [-s, c]])
        inv[a] = np.block([[c.T, -s.T], [s.T, c.T]]) * (2.0 / length)
    for slot, a in ((0, 0), (1, n)):
        c, s = np.cos(angle(a))[:half], np.sin(angle(a))[:half]
        weight = np.full((half, 1), 2.0 / length)
        re_rows = slice(slot * half, (slot + 1) * half)
        im_rows = slice(rows + slot * half, rows + (slot + 1) * half)
        cols = slice(slot * rows, (slot + 1) * rows)
        im = -s
        if slot == 0:
            im = im.copy()
            im[0] = np.cos(np.pi * np.arange(rows))
            weight[0] = 1.0 / length
        fwd[0, re_rows, cols] = c
        fwd[0, im_rows, cols] = im
        inv[0, cols, re_rows] = (c * weight).T
        inv[0, cols, im_rows] = (im * weight).T
    return fwd, inv


def scaled(coef, x):
    if abs(coef - 1.0) < 1e-12:
        return x
    if abs(coef + 1.0) < 1e-12:
        return -x
    return x * np.float32(coef)


def combine(terms, zero):
    total = None
    for coef, x in terms:
        if abs(coef) < 1e-12:
            continue
        if total is None:
            total = scaled(coef, x)
        elif coef < 0:
            total = total - scaled(-coef, x)
        else:
            total = total + scaled(coef, x)
    return zero if total is None else total


def kernel(
    n, nsec, chunk, steps,
    gq_hbm, gk_hbm, vi_hbm, fr_hbm, go_hbm, rate_hbm, skip_hbm, fwd_hbm, inv_hbm,
    oq_hbm, ok_hbm, op_ref, of_hbm, orate_hbm, oskip_hbm,
    gq_ref, gk_ref, vi_ref, fr_ref, go_ref, rate_ref, skip_ref, fwd_ref, inv_ref,
    ostage, zeros, orate_ref, oskip_ref, in_sem, row_sem, out_sem, end_sem,
    sbuf, rbuf, obuf, hbuf, pbuf, part, fold, sstat, gstat,
    s_send, s_recv, o_send, o_recv, p_send, p_recv, t_send, t_recv,
):
    rows = gq_ref.shape[0]
    width = chunk * steps
    seq = rows * n
    me = lax.axis_index("ctx")
    sec = lax.axis_index("section")
    before = lax.rem(sec + nsec - 1, nsec)
    after = lax.rem(sec + 1, nsec)

    def columns(owner, k):
        return pl.ds(pl.multiple_of(owner * width + k * chunk, chunk), chunk)

    tokens = (
        (gk_hbm, gk_ref), (vi_hbm, vi_ref), (gq_hbm, gq_ref), (go_hbm, go_ref), (fr_hbm, fr_ref)
    )
    whole = (
        (rate_hbm, rate_ref), (skip_hbm, skip_ref), (fwd_hbm, fwd_ref), (inv_hbm, inv_ref)
    )

    def load_first(g, d):
        hbm, ref = tokens[g]
        return pltpu.make_async_copy(
            hbm.at[:, columns(d, 0)], ref.at[:, columns(d, 0)], in_sem.at[g, 0, d]
        )

    def load_rest(g, d):
        hbm, ref = tokens[g]
        cols = pl.ds(pl.multiple_of(d * width + chunk, chunk), width - chunk)
        return pltpu.make_async_copy(hbm.at[:, cols], ref.at[:, cols], in_sem.at[g, 1, d])

    def load_whole(g):
        return pltpu.make_async_copy(whole[g][0], whole[g][1], row_sem.at[g])

    load_whole(0).start()
    for o in range(n):
        for g in range(5):
            load_first(g, lax.rem(me + 1 + o, n)).start()
    if steps > 1:
        for d in range(n):
            for g in range(5):
                load_rest(g, d).start()
    for g in range(1, 4):
        load_whole(g).start()

    barrier = pltpu.get_barrier_semaphore()
    for o in range(1, n):
        pl.semaphore_signal(
            barrier, inc=1, device_id={"ctx": lax.rem(me + o, n)}, device_id_type=MESH
        )

    @pl.when(sec < nsec - 1)
    def _():
        pl.semaphore_signal(barrier, inc=1, device_id={"section": after}, device_id_type=MESH)

    @pl.when(sec > 0)
    def _():
        pl.semaphore_wait(barrier, n)

    @pl.when(sec == 0)
    def _():
        pl.semaphore_wait(barrier, n - 1)

    load_whole(0).wait()

    def here(row0, count):
        row = lax.broadcasted_iota(jnp.int32, (count, 1), 0) + (row0 + me * rows)
        return row.astype(F32) * np.float32(1.0 / seq)

    def send_in(k, d):
        return pltpu.make_async_remote_copy(
            src_ref=sbuf.at[k, d], dst_ref=rbuf.at[k, me], send_sem=s_send.at[k, d],
            recv_sem=s_recv.at[k, me], device_id={"ctx": d}, device_id_type=MESH,
        )

    def got_in(k, m):
        return pltpu.make_async_remote_copy(
            src_ref=sbuf.at[k, m], dst_ref=rbuf.at[k, m], send_sem=s_send.at[k, m],
            recv_sem=s_recv.at[k, m], device_id={"ctx": m}, device_id_type=MESH,
        )

    def send_out(k, m):
        return pltpu.make_async_remote_copy(
            src_ref=obuf.at[k, m], dst_ref=hbuf.at[k, me], send_sem=o_send.at[k, m],
            recv_sem=o_recv.at[k, me], device_id={"ctx": m}, device_id_type=MESH,
        )

    def got_out(k, m):
        return pltpu.make_async_remote_copy(
            src_ref=obuf.at[k, m], dst_ref=hbuf.at[k, m], send_sem=o_send.at[k, m],
            recv_sem=o_recv.at[k, m], device_id={"ctx": m}, device_id_type=MESH,
        )

    def send_stat(d):
        return pltpu.make_async_remote_copy(
            src_ref=sstat, dst_ref=gstat.at[me], send_sem=t_send.at[d],
            recv_sem=t_recv.at[me], device_id={"ctx": d}, device_id_type=MESH,
        )

    def got_stat(m):
        return pltpu.make_async_remote_copy(
            src_ref=sstat, dst_ref=gstat.at[m], send_sem=t_send.at[m],
            recv_sem=t_recv.at[m], device_id={"ctx": m}, device_id_type=MESH,
        )

    def pass_copy(k, m):
        return pltpu.make_async_remote_copy(
            src_ref=pbuf.at[k, m], dst_ref=op_ref.at[:, columns(m, k)], send_sem=p_send.at[k, m],
            recv_sem=p_recv.at[k, m], device_id={"section": before}, device_id_type=MESH,
        )

    @pl.loop(0, steps * n)
    def _(i):
        k, o = i // n, lax.rem(i, n)
        d = lax.rem(me + 1 + o, n)
        cols = columns(d, k)

        @pl.when(k == 0)
        def _():
            for g in range(5):
                load_first(g, d).wait()

        if steps > 1:
            @pl.when(k == 1)
            def _():
                for g in range(5):
                    load_rest(g, d).wait()

        mixed = (gk_ref[:, cols].astype(F32) * vi_ref[:, cols].astype(F32)).astype(BF16)
        pulled = (gq_ref[:, cols].astype(F32) * go_ref[:, cols].astype(F32)).astype(BF16)
        envelope = jnp.exp(-rate_ref[:, cols] * here(0, rows))
        filt = (fr_ref[:, cols].astype(F32) * envelope).astype(BF16)
        sbuf[k, d, :, 0:chunk] = mixed
        sbuf[k, d, :, chunk:2 * chunk] = filt
        sbuf[k, d, :, 2 * chunk:3 * chunk] = pulled

        @pl.when(o < n - 1)
        def _():
            send_in(k, d).start()

        @pl.when(o == n - 1)
        def _():
            rbuf[k, me, :, 0:chunk] = mixed
            rbuf[k, me, :, chunk:2 * chunk] = filt
            rbuf[k, me, :, 2 * chunk:3 * chunk] = pulled

    def clear():
        return pltpu.make_async_copy(zeros, op_ref, end_sem.at[0])

    @pl.when(sec == nsec - 1)
    def _():
        zeros[...] = jnp.zeros_like(zeros)
        clear().start()

    for g in range(1, 4):
        load_whole(g).wait()

    def store(g, k, m):
        out = (oq_hbm, ok_hbm, of_hbm)[g]
        return pltpu.make_async_copy(
            ostage.at[g, k, m], out.at[:, columns(m, k)], out_sem.at[g, k, m]
        )

    tile = 16
    top = lax.broadcasted_iota(jnp.int32, (rows, 1), 0)

    @pl.loop(0, steps)
    def _(k):
        @pl.loop(0, n - 1)
        def _(o):
            got_in(k, lax.rem(me + 1 + o, n)).wait_recv()

        @pl.loop(0, rows // tile)
        def _(t):
            at = pl.ds(pl.multiple_of(t * tile, tile), tile)
            low = pl.ds(pl.multiple_of(rows + t * tile, tile), tile)
            for g in range(3):
                lanes = slice(g * chunk, (g + 1) * chunk)
                x = [rbuf[k, m, at, lanes].astype(F32) for m in range(n)]
                zero = jnp.zeros_like(x[0])
                even = combine([(1.0, x[m]) for m in range(0, n, 2)], zero)
                odd = combine([(1.0, x[m]) for m in range(1, n, 2)], zero)
                part[0, at, lanes] = (even + odd).astype(BF16)
                part[0, low, lanes] = (even - odd).astype(BF16)
                for a in range(1, n // 2 + 1):
                    cos = [math.cos(math.pi * m * a / n) for m in range(n)]
                    sin = [math.sin(math.pi * m * a / n) for m in range(n)]
                    ce = combine([(cos[m], x[m]) for m in range(0, n, 2)], zero)
                    co = combine([(cos[m], x[m]) for m in range(1, n, 2)], zero)
                    se = combine([(sin[m], x[m]) for m in range(0, n, 2)], zero)
                    so = combine([(sin[m], x[m]) for m in range(1, n, 2)], zero)
                    part[a, at, lanes] = (ce + co).astype(BF16)
                    part[a, low, lanes] = (-se - so).astype(BF16)
                    if n - a != a:
                        part[n - a, at, lanes] = (ce - co).astype(BF16)
                        part[n - a, low, lanes] = (se - so).astype(BF16)

        @pl.loop(0, n)
        def _(a):
            spec = jnp.dot(fwd_ref[a], part[a], preferred_element_type=F32)
            mr, fr, pr = (spec[:rows, g * chunk:(g + 1) * chunk] for g in range(3))
            mi, fi, pi = (spec[rows:, g * chunk:(g + 1) * chunk] for g in range(3))
            real_pair = jnp.logical_and(top == 0, a == 0)

            def product(ar, ai, br, bi, sign):
                cross = ai * bi
                re = ar * br + jnp.where(real_pair, 0.0, sign * cross)
                im = jnp.where(real_pair, cross, ar * bi - sign * ai * br)
                return re, im

            outs = (
                product(fr, fi, mr, mi, -1.0),
                product(fr, fi, pr, pi, 1.0),
                product(mr, mi, pr, pi, 1.0),
            )
            for g in range(3):
                lanes = slice(g * chunk, (g + 1) * chunk)
                part[a, 0:rows, lanes] = outs[g][0].astype(BF16)
                part[a, rows:2 * rows, lanes] = outs[g][1].astype(BF16)
            fold[a] = jnp.dot(inv_ref[a], part[a], preferred_element_type=F32)

        def unfold(t, carry):
            rate_sum, skip_sum = carry
            at = pl.ds(pl.multiple_of(t * tile, tile), tile)
            low = pl.ds(pl.multiple_of(rows + t * tile, tile), tile)
            for g in range(3):
                lanes = slice(g * chunk, (g + 1) * chunk)
                re = [fold[a, at, lanes] for a in range(n)]
                im = [fold[a, low, lanes] for a in range(n)]
                zero = jnp.zeros_like(re[0])
                for m in range(n):
                    terms = [(1.0, re[0]), ((-1.0) ** m, im[0])]
                    for a in range(1, n):
                        terms.append((math.cos(math.pi * m * a / n), re[a]))
                        terms.append((-math.sin(math.pi * m * a / n), im[a]))
                    value = combine(terms, zero).astype(BF16)
                    obuf[k, m, at, lanes] = value
                    if g == 2:
                        when = lax.broadcasted_iota(jnp.int32, (tile, 1), 0) + (t * tile + m * rows)
                        when = when.astype(F32) * np.float32(1.0 / seq)
                        mixed = rbuf[k, m, at, 0:chunk].astype(F32)
                        filt = rbuf[k, m, at, chunk:2 * chunk].astype(F32)
                        pulled = rbuf[k, m, at, 2 * chunk:3 * chunk].astype(F32)
                        rate_sum = rate_sum + when * value.astype(F32) * filt
                        skip_sum = skip_sum + mixed * pulled
            return rate_sum, skip_sum

        start = jnp.zeros((tile, chunk), F32)
        rate_sum, skip_sum = lax.fori_loop(0, rows // tile, unfold, (start, start))
        mine = pl.ds(pl.multiple_of(k * chunk, chunk), chunk)
        sstat[0:1, mine] = -jnp.sum(rate_sum, axis=0, keepdims=True)
        sstat[1:2, mine] = jnp.sum(skip_sum, axis=0, keepdims=True)

        @pl.loop(0, n - 1)
        def _(o):
            send_out(k, lax.rem(me + 1 + o, n)).start()

        hbuf[k, me] = obuf[k, me]

    for o in range(1, n):
        send_stat(lax.rem(me + o, n)).start()
    gstat[me] = sstat[...]

    @pl.loop(0, steps * n)
    def _(i):
        k, o = i // n, lax.rem(i, n)
        m = lax.rem(me + o, n)

        @pl.when(o > 0)
        def _():
            got_out(k, m).wait_recv()

        cols = columns(m, k)
        conv = hbuf[k, m, :, 0:chunk].astype(F32)
        adjoint = hbuf[k, m, :, chunk:2 * chunk].astype(F32)
        corr = hbuf[k, m, :, 2 * chunk:3 * chunk].astype(F32)
        mixed = sbuf[k, m, :, 0:chunk].astype(F32)
        pulled = sbuf[k, m, :, 2 * chunk:3 * chunk].astype(F32)
        skip = skip_ref[:, cols]
        ostage[0, k, m] = (go_ref[:, cols].astype(F32) * (conv + skip * mixed)).astype(BF16)
        mixed_grad = adjoint + skip * pulled
        pbuf[k, m] = (mixed_grad * gk_ref[:, cols].astype(F32)).astype(BF16)

        @pl.when(sec > 0)
        def _():
            pass_copy(k, m).start()

        store(0, k, m).start()
        ostage[1, k, m] = (mixed_grad * vi_ref[:, cols].astype(F32)).astype(BF16)
        store(1, k, m).start()
        envelope = jnp.exp(-rate_ref[:, cols] * here(0, rows))
        ostage[2, k, m] = (corr * envelope).astype(BF16)
        store(2, k, m).start()

    for o in range(1, n):
        got_stat(lax.rem(me + o, n)).wait_recv()
    for m in range(n):
        orate_ref[:, m * width:(m + 1) * width] = gstat[m, 0:1, :]
        oskip_ref[:, m * width:(m + 1) * width] = gstat[m, 1:2, :]
    rows_out = (
        pltpu.make_async_copy(orate_ref, orate_hbm, end_sem.at[1]),
        pltpu.make_async_copy(oskip_ref, oskip_hbm, end_sem.at[2]),
    )
    for copy in rows_out:
        copy.start()

    for o in range(1, n):
        send_stat(lax.rem(me + o, n)).wait_send()

    @pl.loop(0, steps * (n - 1))
    def _(i):
        k, o = i // (n - 1), lax.rem(i, n - 1)
        d = lax.rem(me + 1 + o, n)
        send_in(k, d).wait_send()
        send_out(k, d).wait_send()

    @pl.loop(0, steps * n)
    def _(i):
        k, m = i // n, lax.rem(i, n)

        @pl.when(sec > 0)
        def _():
            pass_copy(k, m).wait_send()

        @pl.when(sec < nsec - 1)
        def _():
            pass_copy(k, m).wait_recv()

        for g in range(3):
            store(g, k, m).wait()

    for copy in rows_out:
        copy.wait()

    @pl.when(sec == nsec - 1)
    def _():
        clear().wait()


def finish(pieces, *refs):
    count = (len(refs) - 2) // 3
    load_sem, store_sem = refs[-2:]
    copies = []
    for g in range(count):
        src, dst, held = refs[g], refs[count + g], refs[2 * count + g]
        parts = pieces if src.shape[0] % pieces == 0 else 1
        size = src.shape[0] // parts
        for p in range(parts):
            at = pl.ds(p * size, size)
            copies.append((
                pltpu.make_async_copy(src.at[at], held.at[at], load_sem.at[g, p]),
                pltpu.make_async_copy(held.at[at], dst.at[at], store_sem.at[g, p]),
            ))
    for load, _ in copies:
        load.start()
    for load, store in copies:
        load.wait()
        store.start()
    for _, store in copies:
        store.wait()


def shards(n, nsec, gate_q, gate_k, value_in, filter_raw, decay_rate, skip_gain, grad_out):
    rows, channels = gate_q.shape[1:]
    width = channels // n
    chunk = 128
    steps = width // chunk
    fwd, inv = make_tables(n, rows)
    fwd, inv = jnp.asarray(fwd, BF16), jnp.asarray(inv, BF16)
    block = jax.ShapeDtypeStruct((rows, channels), BF16)
    row = jax.ShapeDtypeStruct((1, channels), F32)
    message = (steps, n, rows, 3 * chunk)
    dma = pltpu.SemaphoreType.DMA
    anywhere = pl.BlockSpec(memory_space=pl.ANY)
    shapes = (block, block, block, block, row, row)
    outs = pl.pallas_call(
        functools.partial(kernel, n, nsec, chunk, steps),
        out_shape=shapes,
        in_specs=[anywhere] * 9,
        out_specs=(anywhere,) * 6,
        scratch_shapes=[
            *([pltpu.VMEM((rows, channels), BF16)] * 5),
            *([pltpu.VMEM((1, channels), F32)] * 2),
            *([pltpu.VMEM(fwd.shape, BF16)] * 2),
            pltpu.VMEM((3, steps, n, rows, chunk), BF16),
            pltpu.VMEM((rows, channels), BF16),
            *([pltpu.VMEM((1, channels), F32)] * 2),
            dma((5, 2, n)), dma((4,)), dma((3, steps, n)), dma((3,)),
            pltpu.VMEM(message, BF16),
            pltpu.VMEM(message, BF16),
            pltpu.VMEM(message, BF16),
            pltpu.VMEM(message, BF16),
            pltpu.VMEM((steps, n, rows, chunk), BF16),
            pltpu.VMEM((n, 2 * rows, 3 * chunk), BF16),
            pltpu.VMEM((n, 2 * rows, 3 * chunk), F32),
            pltpu.VMEM((2, width), F32),
            pltpu.VMEM((n, 2, width), F32),
            dma((steps, n)), dma((steps, n)), dma((steps, n)), dma((steps, n)),
            dma((steps, n)), dma((steps, n)), dma((n,)), dma((n,)),
        ],
        compiler_params=pltpu.CompilerParams(
            collective_id=0, has_side_effects=True, vmem_limit_bytes=58 * 1024 * 1024
        ),
        name="hyena_backward",
    )(
        gate_q[0], gate_k[0], value_in[0], filter_raw[0], grad_out[0],
        decay_rate, skip_gain, fwd, inv,
    )
    pieces = 4
    oq, ok, op, of, orate, oskip = pl.pallas_call(
        functools.partial(finish, pieces),
        out_shape=shapes,
        in_specs=[anywhere] * 6,
        out_specs=(anywhere,) * 6,
        scratch_shapes=[
            *(pltpu.VMEM(shape.shape, shape.dtype) for shape in shapes),
            dma((6, pieces)), dma((6, pieces)),
        ],
        name="hand_over",
    )(*outs)
    return oq[None], ok[None], op[None], of[None], orate, oskip


def solution(mesh):
    n, nsec = mesh.shape["ctx"], mesh.shape["section"]
    tokens = P("section", "ctx", None)
    return jax.shard_map(
        functools.partial(shards, n, nsec),
        mesh=mesh,
        in_specs=(tokens, tokens, tokens, tokens, P("section", None), P("section", None), tokens),
        out_specs=(tokens, tokens, tokens, tokens, P("section", None), P("section", None)),
        check_vma=False,
    )
```
